1024 devices in a mesh: cp: 64 (over y, x), grp: 16 (over z, core).
Axes of the slice: x: 8, y: 8, z: 8, core: 2. Of those that a mesh axis runs over, the one named last changes fastest.
Arguments:
- queries: bfloat16 [131072, 2048], P(('cp', 'grp')), may hold values from -6 to 6
- keys: bfloat16 [131072, 512], P(('cp', 'grp')), may hold values from -6 to 6
- values: bfloat16 [131072, 512], P(('cp', 'grp')), may hold values from -6 to 6
- grad_out: bfloat16 [131072, 2048], P(('cp', 'grp')), may hold values from -6 to 6
- segments: int32 [131072], P(('cp', 'grp')), may hold values from 0 to 63, never falling along the last dimension, each value on 1 to 8192 neighbouring positions
- block_ids: int32 [1024, 4], P(('cp', 'grp')), may hold values from 0 to 1023, as said below
- block_count: int32 [1024], P(('cp', 'grp')), may hold values from 1 to 4, as said below
Outputs:
- attended: bfloat16 [131072, 2048], P(('cp', 'grp'))
- grad_queries: bfloat16 [131072, 2048], P(('cp', 'grp'))
- grad_keys: bfloat16 [131072, 512], P(('cp', 'grp'))
- grad_values: bfloat16 [131072, 512], P(('cp', 'grp'))
The draws below stay inside these ranges and needn't reach their ends.
Inputs may be any that keep to these rules, and one draw needn't show every extreme that they name: `block_ids`: row t names tiles of its own neighbourhood (tiles 16 * (t // 16) onward, 16 of them) or of the neighbourhood before it; entry 0 is t itself; the first block_count[t] entries are distinct; later entries are ignored. `block_count`: reaches 4 in every draw.
All inputs are finite; a program needn't handle non-finite values.
Results may differ from the reference program's by a relative error of at most 0.012.
The reference program's roundings to bfloat16 on the way count: a program that leaves them out, or rounds other values in their place, can miss the bound.
Values may be sent and summed in bfloat16 or wider, within the bound.
A program may use at most 64 MiB of HBM per device.

```python
import math
import jax
import jax.numpy as jnp
import numpy as np
from jax import lax

HEADS = 16
KV_HEADS = 4
HEAD = 128
BLOCK = 128
MAXB = 4
GROUP = 16
TILES = 1024
TOKENS = 131072


def draw_queries(key, part):
    normal_part = jnp.clip(jax.random.normal(jax.random.fold_in(key, 1), (TOKENS, HEADS * HEAD), jnp.float32), -6.0, 6.0)
    return normal_part.astype(jnp.bfloat16)


def draw_keys(key, part):
    normal_part = jnp.clip(jax.random.normal(jax.random.fold_in(key, 2), (TOKENS, KV_HEADS * HEAD), jnp.float32), -6.0, 6.0)
    return normal_part.astype(jnp.bfloat16)


def draw_block_ids(key, part):
    tile_count = TILES
    own_tile = jnp.arange(tile_count, dtype=jnp.int32)
    candidate = jnp.arange(2 * GROUP, dtype=jnp.int32)
    named = (own_tile[:, None] // GROUP - 1) * GROUP + candidate[None, :]
    usable = (named >= 0) & (named != own_tile[:, None])
    noise = jax.random.randint(jax.random.fold_in(key, 5), (tile_count, 2 * GROUP), 0, 2 ** 20)
    scores = jnp.where(usable, noise * (2 * GROUP) + candidate[None, :], -1 - candidate[None, :])
    ranking = jnp.argsort(-scores, axis=1, stable=True)[:, :MAXB - 1]
    chosen = jnp.take_along_axis(named, ranking, axis=1)
    chosen_ok = jnp.take_along_axis(usable, ranking, axis=1)
    chosen = jnp.where(chosen_ok, chosen, own_tile[:, None])
    return jnp.concatenate([own_tile[:, None], chosen], axis=1).astype(jnp.int32)


def draw_block_count(key, part):
    tile_count = TILES
    own_tile = jnp.arange(tile_count, dtype=jnp.int32)
    heavy = jax.random.randint(jax.random.fold_in(key, 6), (tile_count,), 0, 4) == 0
    light = 1 + jax.random.randint(jax.random.fold_in(key, 7), (tile_count,), 0, 5)
    used = jnp.where(heavy, MAXB, jnp.minimum(light, MAXB))
    used = jnp.where(own_tile < GROUP, jnp.minimum(used, GROUP), used)
    used = used.at[tile_count - 1].set(MAXB)
    return used.astype(jnp.int32)


def block_levels(key, extent, cuts, low, high):
    def one(dim, shards_of):
        steps = jax.random.uniform(jax.random.fold_in(jax.random.fold_in(key, 6), dim), (shards_of,), jnp.float32, low / len(cuts), high / len(cuts))
        return jnp.repeat(jnp.exp(steps), extent[dim] // shards_of).reshape((-1,) + (1,) * (len(extent) - dim - 1))

    gain = one(*cuts[0])
    for cut in cuts[1:]:
        gain = gain * one(*cut)
    return gain


def profile(number_of, total, reach, lean):
    weights = [(1 << 20) // math.isqrt(standing ** lean) + 1 for standing in range(2, number_of + 1)]
    surplus, given = total - reach - (number_of - 1), [1] * (number_of - 1)
    while surplus > 0:
        movable = [i for i in range(number_of - 1) if given[i] < reach]
        mass, remaining = sum([weights[i] for i in movable]), surplus
        for i in movable:
            extra = min(reach - given[i], max(1, remaining * weights[i] // mass), surplus)
            given[i] = given[i] + extra
            surplus = surplus - extra
    return np.array([reach] + given)


def ragged_sizes(key, amount, total, reach, lean):
    if amount == 2:
        one = jax.random.randint(key, (), max(1, total - reach), min(reach, total - 1) + 1)
        return jnp.stack([one, total - one])
    tallies = jnp.asarray(profile(amount, total, reach, lean), jnp.int32)
    pairs = (amount - 1) // 2
    source_of, receiver = tallies[1:1 + 2 * pairs:2], tallies[2:2 + 2 * pairs:2]
    margin = jnp.minimum(source_of - 1, reach - receiver)
    shifted = jax.random.randint(jax.random.fold_in(key, 1), (pairs,), 0, 1 << 20) % (margin + 1)
    tallies = tallies.at[1:1 + 2 * pairs:2].set(source_of - shifted).at[2:2 + 2 * pairs:2].set(receiver + shifted)
    return tallies[jax.random.permutation(jax.random.fold_in(key, 2), amount)]


def centred(rng, extent, spread, reach, cuts=(), held_as=jnp.bfloat16):
    entries = jax.random.normal(rng, extent, jnp.float32) * spread
    if len(cuts) > 0:
        entries = block_levels(rng, extent, cuts, -0.22, 0.18) * entries
    return jnp.clip(entries, min=-reach, max=reach).astype(held_as)


def setup_inputs(seed: int = 0) -> dict:
    splits = jax.random.split(jax.random.key(seed), 8)
    return {
        "queries": draw_queries(jax.random.fold_in(splits[7], 71), 0),
        "keys": draw_keys(jax.random.fold_in(splits[7], 71), 0),
        "values": centred(splits[2], (TOKENS, KV_HEADS * HEAD), 1.0, 6.0, ((0, 1024),)),
        "grad_out": centred(splits[3], (TOKENS, HEADS * HEAD), 1.0, 6.0, ((0, 1024),)),
        "segments": jnp.searchsorted(jnp.cumsum(ragged_sizes(splits[4], max(TOKENS // (16 * BLOCK), 4), TOKENS, min(64 * BLOCK, TOKENS // 2), 2)), jnp.arange(TOKENS), side="right").astype(jnp.int32),
        "block_ids": draw_block_ids(jax.random.fold_in(splits[7], 71), 0),
        "block_count": draw_block_count(jax.random.fold_in(splits[7], 71), 0),
    }


NEG = -1.0e30


def attend_tile(query, grad_out, tile_keys, tile_values, query_seg, key_seg, is_live, kv_heads):
    tile_rows, full_width = query.shape
    slot_count, tile_size, kv_width = tile_keys.shape
    head_size = kv_width // kv_heads
    group_size = full_width // kv_width
    scaling = head_size ** -0.5
    key_slots = slot_count * tile_size
    allowed = (query_seg[:, None] == key_seg.reshape(key_slots)[None, :]) & jnp.repeat(is_live, tile_size)[None, :]
    query_heads = query.reshape(tile_rows, kv_heads, group_size, head_size).transpose(1, 0, 2, 3)
    grad_heads = grad_out.reshape(tile_rows, kv_heads, group_size, head_size).transpose(1, 0, 2, 3)
    key_heads = tile_keys.reshape(key_slots, kv_heads, head_size).transpose(1, 0, 2)
    value_heads = tile_values.reshape(key_slots, kv_heads, head_size).transpose(1, 0, 2)

    def per_head(pieces):
        query_one, grad_one, key_one, value_one = pieces
        query_f = query_one.astype(jnp.float32)
        grad_f = grad_one.astype(jnp.float32)
        key_f = key_one.astype(jnp.float32)
        value_f = value_one.astype(jnp.float32)
        scores = jnp.einsum("bge,ne->gbn", query_f, key_f) * scaling
        scores = jnp.where(allowed[None], scores, NEG)
        probability = jnp.exp(scores - jnp.max(scores, axis=-1, keepdims=True))
        probability = probability / jnp.sum(probability, axis=-1, keepdims=True)
        weights = lax.optimization_barrier(probability.astype(jnp.bfloat16)).astype(jnp.float32)
        attended = jnp.einsum("gbn,ne->bge", weights, value_f).astype(jnp.bfloat16)
        row_delta = jnp.sum(lax.optimization_barrier(attended).astype(jnp.float32) * grad_f, axis=-1)
        dprobs = jnp.einsum("bge,ne->gbn", grad_f, value_f)
        dscores = probability * (dprobs - row_delta.T[:, :, None])
        dscores = lax.optimization_barrier(dscores.astype(jnp.bfloat16)).astype(jnp.float32)
        grad_query = (jnp.einsum("gbn,ne->bge", dscores, key_f) * scaling).astype(jnp.bfloat16)
        key_term = jnp.einsum("gbn,bge->ne", dscores, query_f) * scaling
        value_term = jnp.einsum("gbn,bge->ne", weights, grad_f)
        return attended, grad_query, key_term, value_term

    attended, grad_query, key_term, value_term = lax.map(per_head, (query_heads, grad_heads, key_heads, value_heads))
    attended = attended.transpose(1, 0, 2, 3).reshape(tile_rows, full_width)
    grad_query = grad_query.transpose(1, 0, 2, 3).reshape(tile_rows, full_width)
    key_term = key_term.transpose(1, 0, 2).reshape(slot_count, tile_size, kv_width)
    value_term = value_term.transpose(1, 0, 2).reshape(slot_count, tile_size, kv_width)
    return attended, grad_query, key_term, value_term


def reference(queries, keys, values, grad_out, segments, block_ids, block_count):
    tile_count = TOKENS // BLOCK
    kv_width = keys.shape[1]
    key_tiles = keys.reshape(tile_count, BLOCK, kv_width)
    value_tiles = values.reshape(tile_count, BLOCK, kv_width)
    query_tiles = queries.reshape(tile_count, BLOCK, queries.shape[1])
    grad_tiles = grad_out.reshape(tile_count, BLOCK, queries.shape[1])
    seg_tiles = segments.reshape(tile_count, BLOCK)

    def advance(carry, pieces):
        key_sum, value_sum = carry
        query_t, grad_t, listed, used, seg_t = pieces
        is_live = jnp.arange(MAXB, dtype=jnp.int32) < used
        attended, grad_query, key_term, value_term = attend_tile(query_t, grad_t, key_tiles[listed], value_tiles[listed], seg_t, seg_tiles[listed], is_live, KV_HEADS)
        key_sum = key_sum.at[listed].add(lax.optimization_barrier(key_term.astype(jnp.bfloat16)).astype(jnp.float32))
        value_sum = value_sum.at[listed].add(lax.optimization_barrier(value_term.astype(jnp.bfloat16)).astype(jnp.float32))
        return (key_sum, value_sum), (attended, grad_query)

    start = jnp.zeros((tile_count, BLOCK, kv_width), jnp.float32)
    (key_sum, value_sum), (attended, grad_query) = lax.scan(advance, (start, start), (query_tiles, grad_tiles, block_ids, block_count, seg_tiles))
    attended = attended.reshape(TOKENS, queries.shape[1])
    grad_query = grad_query.reshape(TOKENS, queries.shape[1])
    grad_keys = key_sum.reshape(TOKENS, kv_width).astype(jnp.bfloat16)
    grad_values = value_sum.reshape(TOKENS, kv_width).astype(jnp.bfloat16)
    return attended, grad_query, grad_keys, grad_values
```

```python
import functools

import jax
import jax.numpy as jnp
from jax import lax
from jax.experimental import pallas as pl
from jax.experimental.pallas import tpu as pltpu
from jax.sharding import PartitionSpec as P

KV_HEADS = 4
NEG = -1e30
MESH = pl.DeviceIdType.MESH
VMEM = pl.BlockSpec(memory_space=pltpu.VMEM)
SMEM = pl.BlockSpec(memory_space=pltpu.SMEM)


class Place:
    def __init__(self):
        self.columns = lax.axis_size("cp")
        self.group = lax.axis_size("grp")
        self.ring = self.group // 2
        self.half = self.ring // 2
        self.cp = lax.axis_index("cp")
        grp = lax.axis_index("grp")
        self.core = lax.rem(grp, 2)
        self.z = grp // 2
        self.turn = 1 - 2 * self.core
        self.ahead = (self.cp, self.place(1))
        self.behind = (self.cp, self.place(-1))
        self.later = (lax.rem(self.cp + 1, self.columns), grp)
        self.earlier = (lax.rem(self.cp + self.columns - 1, self.columns), grp)
        self.partner = (self.cp, 2 * self.z + 1 - self.core)

    def place(self, offset):
        return 2 * lax.rem(self.z + offset * self.turn + 2 * self.ring, self.ring) + self.core

    def far(self, offset):
        return self.place(offset)

    def near(self, offset):
        return self.group + self.place(offset)

    def greet(self):
        barrier = pltpu.get_barrier_semaphore()
        peers = (self.ahead, self.behind, self.later, self.earlier, self.partner)
        for peer in peers:
            pl.semaphore_signal(barrier, inc=1, device_id=peer, device_id_type=MESH)
        pl.semaphore_wait(barrier, len(peers))


def slot_of(ids, count, j, cp, group):
    return jnp.clip(ids[0, j] - (cp - 1) * group, 0, 2 * group - 1)


def gather_kernel(
    ids, count, key_ref, value_ref, seg_ref, chosen_ref, other_ref,
    pool, meta, meta_in, send, recv, psend, precv, msend, mrecv,
):
    me = Place()
    half, group = me.half, me.group
    rows, head = key_ref.shape[0], pool.shape[2]
    kv_heads = key_ref.shape[1] // head
    listed = ids.shape[1]

    own = me.near(0)
    for h in range(kv_heads):
        pool[own, h * rows:(h + 1) * rows, :] = key_ref[:, h * head:(h + 1) * head]
        pool[own, (kv_heads + h) * rows:(kv_heads + h + 1) * rows, :] = value_ref[:, h * head:(h + 1) * head]
    pool[own, 2 * kv_heads * rows:, :] = jnp.broadcast_to(
        seg_ref[...].astype(jnp.float32), (16, rows)
    ).astype(jnp.bfloat16)
    lane = lax.broadcasted_iota(jnp.int32, meta.shape, 1)
    mine = jnp.full(meta.shape, 2 * group, jnp.int32)
    for j in range(listed):
        at = jnp.where(j < count[0], slot_of(ids, count, j, me.cp, group), 2 * group)
        mine = jnp.where(lane == j, at, mine)
    meta[...] = mine

    me.greet()

    def copy(flow, k, source, target, device):
        return pltpu.make_async_remote_copy(
            src_ref=pool.at[source], dst_ref=pool.at[target],
            send_sem=send.at[flow, k], recv_sem=recv.at[flow, k],
            device_id=device, device_id_type=MESH,
        )

    def ahead(k):
        return copy(0, k, me.near(-k), me.near(-k), me.ahead)

    def later(k):
        return copy(1, k, me.near(-k), me.far(-k), me.later)

    def behind(k):
        return copy(2, k, me.far(k), me.far(k), me.behind)

    def earlier(k):
        return copy(3, k, me.far(k), me.near(k), me.earlier)

    def across(slot, n):
        return pltpu.make_async_remote_copy(
            src_ref=pool.at[slot], dst_ref=pool.at[slot],
            send_sem=psend.at[n], recv_sem=precv.at[n],
            device_id=me.partner, device_id_type=MESH,
        )

    meta_copy = pltpu.make_async_remote_copy(
        src_ref=meta, dst_ref=meta_in, send_sem=msend, recv_sem=mrecv,
        device_id=me.partner, device_id_type=MESH,
    )
    started, shared = [], []

    def start(what):
        what.start()
        started.append(what)

    def share(slot):
        what = across(slot, len(shared))
        what.start()
        shared.append(what)

    start(ahead(0))
    start(later(0))
    share(own)
    meta_copy.start()
    for hop in range(half + 1):
        if hop < half:
            ahead(hop).wait_recv()
            if hop + 1 < half:
                start(ahead(hop + 1))
                start(later(hop + 1))
            share(me.near(-hop - 1))
        if hop >= 1:
            behind(hop - 1).wait_recv()
            if hop < half:
                start(behind(hop))
                start(earlier(hop))
            share(me.far(hop))
        if hop < half:
            later(hop).wait_recv()
            if hop == 0:
                start(behind(0))
            share(me.far(-hop))
        if hop >= 2:
            earlier(hop - 1).wait_recv()
            share(me.near(hop - 1))
    for what in started:
        what.wait_send()
    for what in shared:
        what.wait()
    meta_copy.wait()
    other_ref[...] = meta_in[...]
    for j in range(listed):
        chosen_ref[j] = pool[slot_of(ids, count, j, me.cp, group)]


def attend_kernel(
    count, query_ref, grad_ref, key_ref, value_ref, seg_ref, own_ref,
    attended_ref, dquery_ref, terms_ref, bias, weights, dscores,
):
    slots, rows, head = key_ref.shape
    keys = slots * rows
    heads = query_ref.shape[1] // head
    scaling = head ** (-0.5)

    @pl.when(pl.program_id(0) == 0)
    def _():
        asking = jnp.broadcast_to(own_ref[...].astype(jnp.float32), (rows, rows))
        for j in range(slots):
            told = jnp.broadcast_to(seg_ref[j, 0:1, :].astype(jnp.float32), (rows, rows)).T
            live = jnp.where(j < count[0], 0.0, NEG)
            bias[j * rows:(j + 1) * rows, :] = jnp.where(asking == told, live, NEG)

    key = key_ref[...].reshape(keys, head)
    value = value_ref[...].reshape(keys, head)
    key_t, value_t = key.T, value.T
    across = (((1,), (1,)), ((), ()))
    plain = (((1,), (0,)), ((), ()))

    def dot(a, b, dims):
        return lax.dot_general(a, b, dims, preferred_element_type=jnp.float32)

    for g in range(heads):
        at = slice(g * head, (g + 1) * head)
        query, grad = query_ref[:, at], grad_ref[:, at]
        scores = dot(key, query, across) + bias[...]
        raised = jnp.exp((scores - jnp.max(scores, axis=0, keepdims=True)) * scaling)
        probability = raised * (1.0 / jnp.sum(raised, axis=0, keepdims=True))
        weight = probability.astype(jnp.bfloat16)
        dprobs = dot(value, grad, across)
        delta = jnp.sum(weight.astype(jnp.float32) * dprobs, axis=0, keepdims=True)
        dscore = (probability * (dprobs - delta)).astype(jnp.bfloat16)
        weights[:, at] = weight
        dscores[:, at] = dscore
        attended_ref[:, at] = dot(value_t, weight, plain).T.astype(jnp.bfloat16)
        dquery_ref[:, at] = (dot(key_t, dscore, plain).T * scaling).astype(jnp.bfloat16)
    queries = jnp.concatenate([query_ref[:, g * head:(g + 1) * head] for g in range(heads)], axis=0)
    grads = jnp.concatenate([grad_ref[:, g * head:(g + 1) * head] for g in range(heads)], axis=0)
    key_term = (dot(dscores[...], queries, plain) * scaling).astype(jnp.bfloat16)
    value_term = dot(weights[...], grads, plain).astype(jnp.bfloat16)
    for j in range(slots):
        terms_ref[j, 0, 0] = key_term[j * rows:(j + 1) * rows, :]
        terms_ref[j, 0, 1] = value_term[j * rows:(j + 1) * rows, :]
    terms_ref[slots] = jnp.zeros(terms_ref.shape[1:], jnp.bfloat16)


def reduce_kernel(
    ids, count, other, terms, dkey_ref, dvalue_ref,
    given, out, inn, send, recv, psend, precv,
):
    me = Place()
    half, group = me.half, me.group
    listed = ids.shape[1]
    height, head = terms.shape[1:]
    rows = dkey_ref.shape[0]
    given[listed - 1] = jnp.zeros((height, head), jnp.bfloat16)

    mine = [
        jnp.where(j < count[0], slot_of(ids, count, j, me.cp, group), 2 * group) for j in range(listed)
    ]
    theirs = [other[0, j] for j in range(1, listed)]

    me.greet()
    gifts = [
        pltpu.make_async_remote_copy(
            src_ref=terms.at[j], dst_ref=given.at[j - 1], send_sem=psend.at[j - 1], recv_sem=precv.at[j - 1],
            device_id=me.partner, device_id_type=MESH,
        )
        for j in range(1, listed)
    ]
    for gift in gifts:
        gift.start()
    for gift in gifts:
        gift.wait_recv()

    def local(slot):
        a, b = jnp.int32(listed), jnp.int32(listed - 1)
        for j, at in enumerate(mine):
            a = jnp.where(at == slot, j, a)
        for j, at in enumerate(theirs):
            b = jnp.where(at == slot, j, b)
        return a, b

    def total(slot, arrived, piece):
        a, b = local(slot)
        sums = terms[a, piece, :].astype(jnp.float32) + given[b, piece, :].astype(jnp.float32)
        for flow, k in arrived:
            sums = sums + inn[flow, k, piece, :].astype(jnp.float32)
        return sums.astype(jnp.bfloat16)

    def copy(flow, source, target, device):
        return pltpu.make_async_remote_copy(
            src_ref=out.at[flow, source], dst_ref=inn.at[flow, target],
            send_sem=send.at[flow, source], recv_sem=recv.at[flow, target],
            device_id=device, device_id_type=MESH,
        )

    def mover(flow, k):
        if flow == 0:
            return copy(0, k - 1, k - 1, me.behind)
        if flow == 1:
            return copy(1, k, k, me.earlier)
        if flow == 2:
            return copy(2, k - 1, k - 1, me.ahead)
        return copy(3, k, k, me.later)

    started = []

    def pass_on(flow, k, slot, arrived):
        what = mover(flow, k)
        held = k - 1 if flow in (0, 2) else k

        def step(r, _):
            piece = pl.ds(pl.multiple_of(r * rows, rows), rows)
            out[flow, held, piece, :] = total(slot, arrived, piece)
            return _

        lax.fori_loop(0, height // rows, step, 0)
        what.start()
        started.append(what)

    def arrival(flow, k):
        mover(flow, k + 1 if flow in (0, 2) else k).wait_recv()
        return flow, k

    pass_on(0, half, me.near(-half), ())
    pass_on(2, half, me.far(half), ())
    for k in range(half - 1, 0, -1):
        pass_on(3, k, me.near(k), ())
        pass_on(1, k, me.far(-k), ())
    for k in range(half - 1, 0, -1):
        pass_on(2, k, me.far(k), (arrival(2, k), arrival(3, k)))
        pass_on(0, k, me.near(-k), (arrival(0, k), arrival(1, k)))
    pass_on(1, 0, me.far(0), (arrival(2, 0),))
    arrived = (arrival(0, 0), arrival(1, 0))
    for part in range(height // rows):
        sums = total(me.near(0), arrived, slice(part * rows, (part + 1) * rows))
        h, which = part // 2, part % 2
        target = dvalue_ref if which else dkey_ref
        target[:, h * head:(h + 1) * head] = sums
    for what in started:
        what.wait_send()
    for gift in gifts:
        gift.wait_send()


def body(queries, keys, values, grad_out, segments, block_ids, block_count):
    rows = queries.shape[0]
    listed = block_ids.shape[1]
    head = keys.shape[1] // KV_HEADS
    width = queries.shape[1] // KV_HEADS
    group = lax.axis_size("grp")
    half = group // 4
    seg_row = segments.reshape(1, rows)
    packed = 2 * KV_HEADS * rows + 16
    dma = pltpu.SemaphoreType.DMA
    chosen, other = pl.pallas_call(
        gather_kernel,
        out_shape=(
            jax.ShapeDtypeStruct((listed, packed, head), jnp.bfloat16),
            jax.ShapeDtypeStruct((8, 128), jnp.int32),
        ),
        in_specs=[SMEM, SMEM, VMEM, VMEM, VMEM],
        out_specs=(VMEM, VMEM),
        scratch_shapes=[
            pltpu.VMEM((2 * group, packed, head), jnp.bfloat16),
            pltpu.VMEM((8, 128), jnp.int32),
            pltpu.VMEM((8, 128), jnp.int32),
            dma((4, half)),
            dma((4, half)),
            dma((group,)),
            dma((group,)),
            dma,
            dma,
        ],
        compiler_params=pltpu.CompilerParams(collective_id=0, has_side_effects=True),
        name="gather_tiles",
    )(block_ids, block_count, keys, values, seg_row)

    attended, grad_query, terms = pl.pallas_call(
        attend_kernel,
        grid=(KV_HEADS,),
        out_shape=(
            jax.ShapeDtypeStruct(queries.shape, jnp.bfloat16),
            jax.ShapeDtypeStruct(queries.shape, jnp.bfloat16),
            jax.ShapeDtypeStruct((listed + 1, KV_HEADS, 2, rows, head), jnp.bfloat16),
        ),
        in_specs=[
            SMEM,
            pl.BlockSpec((rows, width), lambda h: (0, h)),
            pl.BlockSpec((rows, width), lambda h: (0, h)),
            pl.BlockSpec((listed, rows, head), lambda h: (0, h, 0)),
            pl.BlockSpec((listed, rows, head), lambda h: (0, KV_HEADS + h, 0)),
            pl.BlockSpec((listed, 16, head), lambda h: (0, 2 * KV_HEADS * rows // 16, 0)),
            pl.BlockSpec((1, rows), lambda h: (0, 0)),
        ],
        out_specs=(
            pl.BlockSpec((rows, width), lambda h: (0, h)),
            pl.BlockSpec((rows, width), lambda h: (0, h)),
            pl.BlockSpec((listed + 1, 1, 2, rows, head), lambda h: (0, h, 0, 0, 0)),
        ),
        scratch_shapes=[
            pltpu.VMEM((listed * rows, rows), jnp.float32),
            pltpu.VMEM((listed * rows, width), jnp.bfloat16),
            pltpu.VMEM((listed * rows, width), jnp.bfloat16),
        ],
        name="attend",
    )(block_count, queries, grad_out, chosen, chosen, chosen, seg_row)

    height = 2 * KV_HEADS * rows
    grad_keys, grad_values = pl.pallas_call(
        reduce_kernel,
        out_shape=(
            jax.ShapeDtypeStruct(keys.shape, jnp.bfloat16),
            jax.ShapeDtypeStruct(values.shape, jnp.bfloat16),
        ),
        in_specs=[SMEM, SMEM, SMEM, VMEM],
        out_specs=(VMEM, VMEM),
        scratch_shapes=[
            pltpu.VMEM((listed, height, head), jnp.bfloat16),
            pltpu.VMEM((4, half, height, head), jnp.bfloat16),
            pltpu.VMEM((4, half, height, head), jnp.bfloat16),
            dma((4, half)),
            dma((4, half)),
            dma((listed - 1,)),
            dma((listed - 1,)),
        ],
        compiler_params=pltpu.CompilerParams(collective_id=1, has_side_effects=True),
        name="reduce_terms",
    )(block_ids, block_count, other, terms.reshape(listed + 1, height, head))
    return attended, grad_query, grad_keys, grad_values


def solution(mesh):
    rows = P(("cp", "grp"), None)
    line = P(("cp", "grp"))
    return jax.shard_map(
        body,
        mesh=mesh,
        in_specs=(rows, rows, rows, rows, line, rows, line),
        out_specs=(rows, rows, rows, rows),
        check_vma=False,
    )
```

```python
import functools

import jax
import jax.numpy as jnp
from jax import lax
from jax.experimental import pallas as pl
from jax.experimental.pallas import tpu as pltpu
from jax.sharding import PartitionSpec as P

KV_HEADS = 4
NEG = -1e30
MESH = pl.DeviceIdType.MESH
VMEM = pl.BlockSpec(memory_space=pltpu.VMEM)
SMEM = pl.BlockSpec(memory_space=pltpu.SMEM)


class Place:
    def __init__(self):
        self.columns = lax.axis_size("cp")
        self.group = lax.axis_size("grp")
        self.ring = self.group // 2
        self.half = self.ring // 2
        self.cp = lax.axis_index("cp")
        grp = lax.axis_index("grp")
        self.core = lax.rem(grp, 2)
        self.z = grp // 2
        self.turn = 1 - 2 * self.core
        self.ahead = (self.cp, self.place(1))
        self.behind = (self.cp, self.place(-1))
        self.later = (lax.rem(self.cp + 1, self.columns), grp)
        self.earlier = (lax.rem(self.cp + self.columns - 1, self.columns), grp)
        self.partner = (self.cp, 2 * self.z + 1 - self.core)

    def place(self, offset):
        return 2 * lax.rem(self.z + offset * self.turn + 2 * self.ring, self.ring) + self.core

    def far(self, offset):
        return self.place(offset)

    def near(self, offset):
        return self.group + self.place(offset)

    def greet(self):
        barrier = pltpu.get_barrier_semaphore()
        peers = (self.ahead, self.behind, self.later, self.earlier, self.partner)
        for peer in peers:
            pl.semaphore_signal(barrier, inc=1, device_id=peer, device_id_type=MESH)
        pl.semaphore_wait(barrier, len(peers))


def slot_of(ids, count, j, cp, group):
    return jnp.clip(ids[0, j] - (cp - 1) * group, 0, 2 * group - 1)


def window_kernel(
    ids, count, key_ref, value_ref, seg_ref, query_any, grad_any,
    attended_any, dquery_any, dkey_ref, dvalue_ref,
    query_ref, grad_ref, attended_ref, dquery_ref, bias, weights, dscores,
    meta, meta_in, other, out, inn, *rest,
):
    pools, terms, given = rest[:KV_HEADS], rest[KV_HEADS:2 * KV_HEADS], rest[2 * KV_HEADS:3 * KV_HEADS]
    gsend, grecv, psend, precv, rsend, rrecv, bsend, brecv, msend, mrecv, load, store, sload = rest[3 * KV_HEADS:]
    me = Place()
    half, ring, group = me.half, me.ring, me.group
    rows = key_ref.shape[0]
    head = key_ref.shape[1] // KV_HEADS
    width = query_ref.shape[1] // KV_HEADS
    listed = ids.shape[1]
    keys = listed * rows
    scaling = head ** (-0.5)

    loads = [
        pltpu.make_async_copy(query_any, query_ref, load.at[0]),
        pltpu.make_async_copy(grad_any, grad_ref, load.at[1]),
    ]
    for what in loads:
        what.start()

    above = [16] + [0] * (KV_HEADS - 1)
    own = me.near(0)
    pools[0][own, 0:16, :] = jnp.broadcast_to(seg_ref[...].astype(jnp.float32), (16, rows)).astype(jnp.bfloat16)
    for h in range(KV_HEADS):
        pools[h][own, above[h]:above[h] + rows, :] = key_ref[:, h * head:(h + 1) * head]
        pools[h][own, above[h] + rows:above[h] + 2 * rows, :] = value_ref[:, h * head:(h + 1) * head]
    slots = [slot_of(ids, count, j, me.cp, group) for j in range(listed)]
    mine = [jnp.where(j < count[0], slots[j], 2 * group) for j in range(listed)]
    lane = lax.broadcasted_iota(jnp.int32, meta.shape, 1)
    told = jnp.full(meta.shape, 2 * group, jnp.int32)
    for j in range(listed):
        told = jnp.where(lane == j, mine[j], told)
    meta[...] = told

    me.greet()

    def remote(source, target, send, recv, device):
        return pltpu.make_async_remote_copy(
            src_ref=source, dst_ref=target, send_sem=send, recv_sem=recv, device_id=device, device_id_type=MESH
        )

    started, shared = [], [[] for _ in range(KV_HEADS)]

    def start(what):
        what.start()
        started.append(what)

    def chain(flow, k, h):
        source, target, device = (
            (me.near(-k), me.near(-k), me.ahead),
            (me.near(-k), me.far(-k), me.later),
            (me.far(k), me.far(k), me.behind),
            (me.far(k), me.near(k), me.earlier),
        )[flow]
        return remote(pools[h].at[source], pools[h].at[target], gsend.at[flow, k, h], grecv.at[flow, k, h], device)

    def share(slot, h):
        n = len(shared[h])
        what = remote(pools[h].at[slot], pools[h].at[slot], psend.at[n, h], precv.at[n, h], me.partner)
        what.start()
        shared[h].append(what)

    def gather_hop(hop, h):
        if hop < half:
            chain(0, hop, h).wait_recv()
            if hop + 1 < half:
                start(chain(0, hop + 1, h))
                start(chain(1, hop + 1, h))
            share(me.near(-hop - 1), h)
        if hop >= 1:
            chain(2, hop - 1, h).wait_recv()
            if hop < half:
                start(chain(2, hop, h))
                start(chain(3, hop, h))
            share(me.far(hop), h)
        if hop < half:
            chain(1, hop, h).wait_recv()
            if hop == 0:
                start(chain(2, 0, h))
            share(me.far(-hop), h)
        if hop >= 2:
            chain(3, hop - 1, h).wait_recv()
            share(me.near(hop - 1), h)

    for h in range(KV_HEADS):
        start(chain(0, 0, h))
        start(chain(1, 0, h))
        share(own, h)
        if h == 0:
            meta_copy = remote(meta, meta_in, msend, mrecv, me.partner)
            meta_copy.start()
    for hop in range(half + 1):
        for h in range(KV_HEADS):
            gather_hop(hop, h)

    meta_copy.wait()
    meta_load = pltpu.make_async_copy(meta_in, other, sload)
    meta_load.start()
    for what in loads:
        what.wait()

    def dot(a, b, dims):
        return lax.dot_general(a, b, (dims, ((), ())), preferred_element_type=jnp.float32)

    across, plain = ((1,), (1,)), ((1,), (0,))

    def attend(h):
        for what in shared[h]:
            what.wait()
        pool, first = pools[h], above[h]
        if h == 0:
            asking = jnp.broadcast_to(seg_ref[...].astype(jnp.float32), (rows, rows))
            for j in range(listed):
                having = jnp.broadcast_to(pool[slots[j], 0:1, :].astype(jnp.float32), (rows, rows)).T
                live = jnp.where(j < count[0], 0.0, NEG)
                bias[j * rows:(j + 1) * rows, :] = jnp.where(asking == having, live, NEG)
        key = jnp.concatenate([pool[slots[j], first:first + rows, :] for j in range(listed)], axis=0)
        value = jnp.concatenate([pool[slots[j], first + rows:first + 2 * rows, :] for j in range(listed)], axis=0)
        key_t, value_t = key.T, value.T
        queries, grads = [], []
        for g in range(width // head):
            at = slice(g * head, (g + 1) * head)
            whole = slice(h * width + g * head, h * width + (g + 1) * head)
            query, grad = query_ref[:, whole], grad_ref[:, whole]
            queries.append(query)
            grads.append(grad)
            scores = dot(key, query, across) + bias[...]
            raised = jnp.exp((scores - jnp.max(scores, axis=0, keepdims=True)) * scaling)
            probability = raised * (1.0 / jnp.sum(raised, axis=0, keepdims=True))
            weight = probability.astype(jnp.bfloat16)
            dprobs = dot(value, grad, across)
            delta = jnp.sum(weight.astype(jnp.float32) * dprobs, axis=0, keepdims=True)
            dscore = (probability * (dprobs - delta)).astype(jnp.bfloat16)
            weights[:, at] = weight
            dscores[:, at] = dscore
            attended_ref[:, whole] = dot(value_t, weight, plain).T.astype(jnp.bfloat16)
            dquery_ref[:, whole] = (dot(key_t, dscore, plain).T * scaling).astype(jnp.bfloat16)
        key_term = (dot(dscores[...], jnp.concatenate(queries, axis=0), plain) * scaling).astype(jnp.bfloat16)
        value_term = dot(weights[...], jnp.concatenate(grads, axis=0), plain).astype(jnp.bfloat16)
        for j in range(listed):
            terms[h][j, 0:rows, :] = key_term[j * rows:(j + 1) * rows, :]
            terms[h][j, rows:2 * rows, :] = value_term[j * rows:(j + 1) * rows, :]

    def mover(flow, k, h):
        at = k - 1 if flow in (0, 2) else k
        device = (me.behind, me.earlier, me.ahead, me.later)[flow]
        return remote(out.at[flow, at, h], inn.at[flow, at, h], rsend.at[flow, at, h], rrecv.at[flow, at, h], device)

    def total(slot, arrived, h):
        a, b = jnp.int32(listed), jnp.int32(listed - 1)
        for j in range(listed):
            a = jnp.where(mine[j] == slot, j, a)
        for j in range(1, listed):
            b = jnp.where(other[0, j] == slot, j - 1, b)
        sums = terms[h][a].astype(jnp.float32) + given[h][b].astype(jnp.float32)
        for flow, k in arrived:
            sums = sums + inn[flow, k, h].astype(jnp.float32)
        return sums.astype(jnp.bfloat16)

    def pass_on(flow, k, h, slot, arrived):
        out[flow, k - 1 if flow in (0, 2) else k, h] = total(slot, arrived, h)
        start(mover(flow, k, h))

    def arrival(flow, k, h):
        mover(flow, k + 1 if flow in (0, 2) else k, h).wait_recv()
        return flow, k

    gifts, stores = {}, []

    def reduce(stage, h):
        if stage == 0:
            for j in range(1, listed):
                gifts[j, h] = remote(
                    terms[h].at[j], given[h].at[j - 1], bsend.at[j - 1, h], brecv.at[j - 1, h], me.partner
                )
                gifts[j, h].start()
        elif stage == 1:
            for j in range(1, listed):
                gifts[j, h].wait_recv()
            pass_on(0, half, h, me.near(-half), ())
            pass_on(2, half, h, me.far(half), ())
            for k in range(half - 1, 0, -1):
                pass_on(3, k, h, me.near(k), ())
                pass_on(1, k, h, me.far(-k), ())
            columns = pl.ds(h * width, width)
            for n, (a, b) in enumerate(((attended_ref, attended_any), (dquery_ref, dquery_any))):
                what = pltpu.make_async_copy(a.at[:, columns], b.at[:, columns], store.at[n, h])
                what.start()
                stores.append(what)
        elif stage <= half:
            k = half + 1 - stage
            pass_on(2, k, h, me.far(k), (arrival(2, k, h), arrival(3, k, h)))
            pass_on(0, k, h, me.near(-k), (arrival(0, k, h), arrival(1, k, h)))
        elif stage == half + 1:
            pass_on(1, 0, h, me.far(0), (arrival(2, 0, h),))
        else:
            sums = total(me.near(0), (arrival(0, 0, h), arrival(1, 0, h)), h)
            dkey_ref[:, h * head:(h + 1) * head] = sums[0:rows, :]
            dvalue_ref[:, h * head:(h + 1) * head] = sums[rows:2 * rows, :]

    for h in range(KV_HEADS):
        terms[h][listed] = jnp.zeros((2 * rows, head), jnp.bfloat16)
        given[h][listed - 1] = jnp.zeros((2 * rows, head), jnp.bfloat16)
    meta_load.wait()
    for turn in range(KV_HEADS + half + 2):
        if turn < KV_HEADS:
            attend(turn)
        for h in range(min(turn, KV_HEADS - 1), max(turn - half - 3, -1), -1):
            reduce(turn - h, h)
    for what in started:
        what.wait_send()
    for what in gifts.values():
        what.wait_send()
    for what in stores:
        what.wait()


def body(queries, keys, values, grad_out, segments, block_ids, block_count):
    rows = queries.shape[0]
    listed = block_ids.shape[1]
    head = keys.shape[1] // KV_HEADS
    width = queries.shape[1] // KV_HEADS
    group = lax.axis_size("grp")
    half = group // 4
    dma = pltpu.SemaphoreType.DMA
    vmem = functools.partial(pltpu.VMEM, dtype=jnp.bfloat16)
    anywhere = pl.BlockSpec(memory_space=pl.ANY)
    return pl.pallas_call(
        window_kernel,
        out_shape=tuple(jax.ShapeDtypeStruct(a.shape, jnp.bfloat16) for a in (queries, queries, keys, values)),
        in_specs=[SMEM, SMEM, VMEM, VMEM, VMEM, anywhere, anywhere],
        out_specs=(anywhere, anywhere, VMEM, VMEM),
        scratch_shapes=[
            vmem(queries.shape), vmem(queries.shape), vmem(queries.shape), vmem(queries.shape),
            pltpu.VMEM((listed * rows, rows), jnp.float32),
            vmem((listed * rows, width)),
            vmem((listed * rows, width)),
            pltpu.VMEM((8, 128), jnp.int32),
            pltpu.VMEM((8, 128), jnp.int32),
            pltpu.SMEM((8, 128), jnp.int32),
            vmem((4, half, KV_HEADS, 2 * rows, head)),
            vmem((4, half, KV_HEADS, 2 * rows, head)),
            vmem((2 * group, 2 * rows + 16, head)),
            *[vmem((2 * group, 2 * rows, head))] * (KV_HEADS - 1),
            *[vmem((listed + 1, 2 * rows, head))] * KV_HEADS,
            *[vmem((listed, 2 * rows, head))] * KV_HEADS,
            dma((4, half, KV_HEADS)), dma((4, half, KV_HEADS)),
            dma((group, KV_HEADS)), dma((group, KV_HEADS)),
            dma((4, half, KV_HEADS)), dma((4, half, KV_HEADS)),
            dma((listed - 1, KV_HEADS)), dma((listed - 1, KV_HEADS)),
            dma, dma, dma((2,)), dma((2, KV_HEADS)), dma,
        ],
        compiler_params=pltpu.CompilerParams(
            collective_id=0, has_side_effects=True, vmem_limit_bytes=60 * 1024 * 1024
        ),
        name="window",
    )(block_ids, block_count, keys, values, segments.reshape(1, rows), queries, grad_out)


def solution(mesh):
    rows = P(("cp", "grp"), None)
    line = P(("cp", "grp"))
    return jax.shard_map(
        body,
        mesh=mesh,
        in_specs=(rows, rows, rows, rows, line, rows, line),
        out_specs=(rows, rows, rows, rows),
        check_vma=False,
    )
```

```python
import functools

import jax
import jax.numpy as jnp
from jax import lax
from jax.experimental import pallas as pl
from jax.experimental.pallas import tpu as pltpu
from jax.sharding import PartitionSpec as P

KV_HEADS = 4
NEG = -1e30
MESH = pl.DeviceIdType.MESH
VMEM = pl.BlockSpec(memory_space=pltpu.VMEM)
SMEM = pl.BlockSpec(memory_space=pltpu.SMEM)


class Place:
    def __init__(self):
        self.columns = lax.axis_size("cp")
        self.group = lax.axis_size("grp")
        self.ring = self.group // 2
        self.half = self.ring // 2
        self.cp = lax.axis_index("cp")
        grp = lax.axis_index("grp")
        self.core = lax.rem(grp, 2)
        self.z = grp // 2
        self.turn = 1 - 2 * self.core
        self.ahead = (self.cp, self.place(1))
        self.behind = (self.cp, self.place(-1))
        self.later = (lax.rem(self.cp + 1, self.columns), grp)
        self.earlier = (lax.rem(self.cp + self.columns - 1, self.columns), grp)
        self.partner = (self.cp, 2 * self.z + 1 - self.core)
        self.peers = (self.ahead, self.behind, self.later, self.earlier, self.partner)

    def place(self, offset):
        return 2 * lax.rem(self.z + offset * self.turn + 2 * self.ring, self.ring) + self.core

    def far(self, offset):
        return self.place(offset)

    def near(self, offset):
        return self.group + self.place(offset)

    def greet(self):
        for peer in self.peers:
            pl.semaphore_signal(pltpu.get_barrier_semaphore(), inc=1, device_id=peer, device_id_type=MESH)

    def met(self):
        pl.semaphore_wait(pltpu.get_barrier_semaphore(), len(self.peers))


def slot_of(ids, count, j, cp, group):
    return jnp.clip(ids[0, j] - (cp - 1) * group, 0, 2 * group - 1)


def window_kernel(
    ids, count, seg_ref, key_any, value_any, query_any, grad_any,
    attended_any, dquery_any, dkey_any, dvalue_any,
    key_ref, value_ref, query_ref, grad_ref, attended_ref, dquery_ref, dkey_ref, dvalue_ref, bias, weights, dscores,
    meta, meta_in, other, out, inn, *rest,
):
    pools, terms, given = rest[:KV_HEADS], rest[KV_HEADS:2 * KV_HEADS], rest[2 * KV_HEADS:3 * KV_HEADS]
    gsend, grecv, psend, precv, rsend, rrecv, bsend, brecv, msend, mrecv, load, store, sload = rest[3 * KV_HEADS:]
    me = Place()
    half, ring, group = me.half, me.ring, me.group
    rows = key_ref.shape[0]
    head = key_ref.shape[1] // KV_HEADS
    width = query_ref.shape[1] // KV_HEADS
    listed = ids.shape[1]
    keys = listed * rows
    scaling = head ** (-0.5)

    me.greet()
    loads = [
        pltpu.make_async_copy(key_any, key_ref, load.at[2]),
        pltpu.make_async_copy(value_any, value_ref, load.at[3]),
        pltpu.make_async_copy(query_any, query_ref, load.at[0]),
        pltpu.make_async_copy(grad_any, grad_ref, load.at[1]),
    ]
    for what in loads:
        what.start()
    for h in range(KV_HEADS):
        terms[h][listed] = jnp.zeros((2 * rows, head), jnp.bfloat16)
        given[h][listed - 1] = jnp.zeros((2 * rows, head), jnp.bfloat16)

    slots = [slot_of(ids, count, j, me.cp, group) for j in range(listed)]
    mine = [jnp.where(j < count[0], slots[j], 2 * group) for j in range(listed)]
    lane = lax.broadcasted_iota(jnp.int32, meta.shape, 1)
    told = jnp.full(meta.shape, 2 * group, jnp.int32)
    for j in range(listed):
        told = jnp.where(lane == j, mine[j], told)
    meta[...] = told

    for what in loads[:2]:
        what.wait()

    above = [16] + [0] * (KV_HEADS - 1)
    own = me.near(0)
    pools[0][own, 0:16, :] = jnp.broadcast_to(seg_ref[...].astype(jnp.float32), (16, rows)).astype(jnp.bfloat16)
    for h in range(KV_HEADS):
        pools[h][own, above[h]:above[h] + rows, :] = key_ref[:, h * head:(h + 1) * head]
        pools[h][own, above[h] + rows:above[h] + 2 * rows, :] = value_ref[:, h * head:(h + 1) * head]

    me.met()

    def remote(source, target, send, recv, device):
        return pltpu.make_async_remote_copy(
            src_ref=source, dst_ref=target, send_sem=send, recv_sem=recv, device_id=device, device_id_type=MESH
        )

    started, shared = [], [[] for _ in range(KV_HEADS)]

    def start(what):
        what.start()
        started.append(what)

    def chain(flow, k, h):
        source, target, device = (
            (me.near(-k), me.near(-k), me.ahead),
            (me.near(-k), me.far(-k), me.later),
            (me.far(k), me.far(k), me.behind),
            (me.far(k), me.near(k), me.earlier),
        )[flow]
        return remote(pools[h].at[source], pools[h].at[target], gsend.at[flow, k, h], grecv.at[flow, k, h], device)

    def share(slot, h):
        n = len(shared[h])
        what = remote(pools[h].at[slot], pools[h].at[slot], psend.at[n, h], precv.at[n, h], me.partner)
        what.start()
        shared[h].append(what)

    def gather_hop(hop, h):
        if hop < half:
            chain(0, hop, h).wait_recv()
            if hop + 1 < half:
                start(chain(0, hop + 1, h))
                start(chain(1, hop + 1, h))
            share(me.near(-hop - 1), h)
        if hop >= 1:
            chain(2, hop - 1, h).wait_recv()
            if hop < half:
                start(chain(2, hop, h))
                start(chain(3, hop, h))
            share(me.far(hop), h)
        if hop < half:
            chain(1, hop, h).wait_recv()
            if hop == 0:
                start(chain(2, 0, h))
            share(me.far(-hop), h)
        if hop >= 2:
            chain(3, hop - 1, h).wait_recv()
            share(me.near(hop - 1), h)

    for h in range(KV_HEADS):
        start(chain(0, 0, h))
        start(chain(1, 0, h))
        share(own, h)
        if h == 0:
            meta_copy = remote(meta, meta_in, msend, mrecv, me.partner)
            meta_copy.start()
    for hop in range(half):
        for h in range(KV_HEADS):
            gather_hop(hop, h)
    for h in range(2):
        gather_hop(half, h)

    meta_copy.wait()
    meta_load = pltpu.make_async_copy(meta_in, other, sload)
    meta_load.start()
    for what in loads[2:]:
        what.wait()

    def dot(a, b, dims):
        return lax.dot_general(a, b, (dims, ((), ())), preferred_element_type=jnp.float32)

    across, plain = ((1,), (1,)), ((1,), (0,))

    transposed = {}

    def attend(h):
        for what in shared[h]:
            what.wait()
        pool, first = pools[h], above[h]
        if h == 0:
            asking = jnp.broadcast_to(seg_ref[...].astype(jnp.float32), (rows, rows))
            for j in range(listed):
                having = jnp.broadcast_to(pool[slots[j], 0:1, :].astype(jnp.float32), (rows, rows)).T
                live = jnp.where(j < count[0], 0.0, NEG)
                bias[j * rows:(j + 1) * rows, :] = jnp.where(asking == having, live, NEG)
        key = jnp.concatenate([pool[slots[j], first:first + rows, :] for j in range(listed)], axis=0)
        value = jnp.concatenate([pool[slots[j], first + rows:first + 2 * rows, :] for j in range(listed)], axis=0)
        transposed[h] = key.T, value.T
        heads = [slice(h * width + at, h * width + at + head) for at in range(0, width, head)]
        queries = [query_ref[:, at] for at in heads]
        grads = [grad_ref[:, at] for at in heads]
        for g in range(0, len(heads), 2):
            at = slice(g * head, (g + 2) * head)
            masked = jnp.concatenate([bias[...]] * 2, axis=1)
            scores = dot(key, jnp.concatenate(queries[g:g + 2], axis=0), across) + masked
            raised = jnp.exp((scores - jnp.max(scores, axis=0, keepdims=True)) * scaling)
            probability = raised * (1.0 / jnp.sum(raised, axis=0, keepdims=True))
            weight = probability.astype(jnp.bfloat16)
            dprobs = dot(value, jnp.concatenate(grads[g:g + 2], axis=0), across)
            delta = jnp.sum(weight.astype(jnp.float32) * dprobs, axis=0, keepdims=True)
            weights[h % 2, :, at] = weight
            dscores[h % 2, :, at] = (probability * (dprobs - delta)).astype(jnp.bfloat16)
        key_term = (dot(dscores[h % 2], jnp.concatenate(queries, axis=0), plain) * scaling).astype(jnp.bfloat16)
        value_term = dot(weights[h % 2], jnp.concatenate(grads, axis=0), plain).astype(jnp.bfloat16)
        for j in range(listed):
            terms[h][j, 0:rows, :] = key_term[j * rows:(j + 1) * rows, :]
            terms[h][j, rows:2 * rows, :] = value_term[j * rows:(j + 1) * rows, :]

    def finish(h):
        key_t, value_t = transposed.pop(h)
        attended = dot(value_t, weights[h % 2], plain).astype(jnp.bfloat16)
        dquery = (dot(key_t, dscores[h % 2], plain) * scaling).astype(jnp.bfloat16)
        for at in range(0, width, head):
            attended_ref[:, h * width + at:h * width + at + head] = attended[:, at:at + head].T
            dquery_ref[:, h * width + at:h * width + at + head] = dquery[:, at:at + head].T

    def mover(flow, k, h):
        at = k - 1 if flow in (0, 2) else k
        device = (me.behind, me.earlier, me.ahead, me.later)[flow]
        return remote(out.at[flow, at, h], inn.at[flow, at, h], rsend.at[flow, at, h], rrecv.at[flow, at, h], device)

    def total(slot, arrived, h):
        a, b = jnp.int32(listed), jnp.int32(listed - 1)
        for j in range(listed):
            a = jnp.where(mine[j] == slot, j, a)
        for j in range(1, listed):
            b = jnp.where(other[0, j] == slot, j - 1, b)
        sums = terms[h][a].astype(jnp.float32) + given[h][b].astype(jnp.float32)
        for flow, k in arrived:
            sums = sums + inn[flow, k, h].astype(jnp.float32)
        return sums.astype(jnp.bfloat16)

    def pass_on(flow, k, h, slot, arrived):
        out[flow, k - 1 if flow in (0, 2) else k, h] = total(slot, arrived, h)
        start(mover(flow, k, h))

    def arrival(flow, k, h):
        mover(flow, k + 1 if flow in (0, 2) else k, h).wait_recv()
        return flow, k

    gifts, stores = {}, []

    def put(n, h, a, b, columns):
        at = slice(h * columns, (h + 1) * columns)
        what = pltpu.make_async_copy(a.at[:, at], b.at[:, at], store.at[n, h])
        what.start()
        stores.append(what)

    def reduce(stage, h):
        if stage == 0:
            for j in range(1, listed):
                gifts[j, h] = remote(
                    terms[h].at[j], given[h].at[j - 1], bsend.at[j - 1, h], brecv.at[j - 1, h], me.partner
                )
                gifts[j, h].start()
        elif stage == 1:
            for j in range(1, listed):
                gifts[j, h].wait_recv()
            pass_on(0, half, h, me.near(-half), ())
            pass_on(2, half, h, me.far(half), ())
            for k in range(half - 1, 0, -1):
                pass_on(3, k, h, me.near(k), ())
                pass_on(1, k, h, me.far(-k), ())
            put(0, h, attended_ref, attended_any, width)
            put(1, h, dquery_ref, dquery_any, width)
        elif stage <= half:
            k = half + 1 - stage
            pass_on(2, k, h, me.far(k), (arrival(2, k, h), arrival(3, k, h)))
            pass_on(0, k, h, me.near(-k), (arrival(0, k, h), arrival(1, k, h)))
        elif stage == half + 1:
            pass_on(1, 0, h, me.far(0), (arrival(2, 0, h),))
        else:
            sums = total(me.near(0), (arrival(0, 0, h), arrival(1, 0, h)), h)
            dkey_ref[:, h * head:(h + 1) * head] = sums[0:rows, :]
            dvalue_ref[:, h * head:(h + 1) * head] = sums[rows:2 * rows, :]
            put(2, h, dkey_ref, dkey_any, head)
            put(3, h, dvalue_ref, dvalue_any, head)

    meta_load.wait()
    for turn in range(KV_HEADS + half + 2):
        if turn < KV_HEADS:
            attend(turn)
            reduce(0, turn)
            finish(turn)
            if turn + 2 < KV_HEADS:
                gather_hop(half, turn + 2)
            reduce(1, turn)
        for h in range(KV_HEADS - 1, -1, -1):
            if 2 <= turn - h <= half + 2:
                reduce(turn - h, h)
    for what in started:
        what.wait_send()
    for what in gifts.values():
        what.wait_send()
    for what in stores:
        what.wait()


def deliver_kernel(*refs):
    sources, targets, held, (load, store) = refs[:4], refs[4:8], refs[8:12], refs[12:]
    ins = [pltpu.make_async_copy(a, b, load.at[n]) for n, (a, b) in enumerate(zip(sources, held))]
    outs = [pltpu.make_async_copy(a, b, store.at[n]) for n, (a, b) in enumerate(zip(held, targets))]
    for what in ins:
        what.start()
    for a, b in zip(ins, outs):
        a.wait()
        b.start()
    for what in outs:
        what.wait()


def body(queries, keys, values, grad_out, segments, block_ids, block_count):
    rows = queries.shape[0]
    listed = block_ids.shape[1]
    head = keys.shape[1] // KV_HEADS
    width = queries.shape[1] // KV_HEADS
    group = lax.axis_size("grp")
    half = group // 4
    dma = pltpu.SemaphoreType.DMA
    vmem = functools.partial(pltpu.VMEM, dtype=jnp.bfloat16)
    anywhere = pl.BlockSpec(memory_space=pl.ANY)
    results = pl.pallas_call(
        window_kernel,
        out_shape=tuple(jax.ShapeDtypeStruct(a.shape, jnp.bfloat16) for a in (queries, queries, keys, values)),
        in_specs=[SMEM, SMEM, VMEM, anywhere, anywhere, anywhere, anywhere],
        out_specs=(anywhere,) * 4,
        scratch_shapes=[
            *[vmem(keys.shape)] * 2, *[vmem(queries.shape)] * 4, *[vmem(keys.shape)] * 2,
            pltpu.VMEM((listed * rows, rows), jnp.float32),
            vmem((2, listed * rows, width)),
            vmem((2, listed * rows, width)),
            pltpu.VMEM((8, 128), jnp.int32),
            pltpu.VMEM((8, 128), jnp.int32),
            pltpu.SMEM((8, 128), jnp.int32),
            vmem((4, half, KV_HEADS, 2 * rows, head)),
            vmem((4, half, KV_HEADS, 2 * rows, head)),
            vmem((2 * group, 2 * rows + 16, head)),
            *[vmem((2 * group, 2 * rows, head))] * (KV_HEADS - 1),
            *[vmem((listed + 1, 2 * rows, head))] * KV_HEADS,
            *[vmem((listed, 2 * rows, head))] * KV_HEADS,
            dma((4, half, KV_HEADS)), dma((4, half, KV_HEADS)),
            dma((group, KV_HEADS)), dma((group, KV_HEADS)),
            dma((4, half, KV_HEADS)), dma((4, half, KV_HEADS)),
            dma((listed - 1, KV_HEADS)), dma((listed - 1, KV_HEADS)),
            dma, dma, dma((4,)), dma((4, KV_HEADS)), dma,
        ],
        compiler_params=pltpu.CompilerParams(
            collective_id=0, has_side_effects=True, vmem_limit_bytes=60 * 1024 * 1024
        ),
        name="window",
    )(block_ids, block_count, segments.reshape(1, rows), keys, values, queries, grad_out)
    return pl.pallas_call(
        deliver_kernel,
        out_shape=tuple(jax.ShapeDtypeStruct(a.shape, a.dtype) for a in results),
        in_specs=[anywhere] * 4,
        out_specs=(anywhere,) * 4,
        scratch_shapes=[*[vmem(a.shape) for a in results], dma((4,)), dma((4,))],
        name="deliver",
    )(*results)


def solution(mesh):
    rows = P(("cp", "grp"), None)
    line = P(("cp", "grp"))
    return jax.shard_map(
        body,
        mesh=mesh,
        in_specs=(rows, rows, rows, rows, line, rows, line),
        out_specs=(rows, rows, rows, rows),
        check_vma=False,
    )
```

```python
import functools

import jax
import jax.numpy as jnp
from jax import lax
from jax.experimental import pallas as pl
from jax.experimental.pallas import tpu as pltpu
from jax.sharding import PartitionSpec as P

KV_HEADS = 4
NEG = -1e30
MESH = pl.DeviceIdType.MESH
VMEM = pl.BlockSpec(memory_space=pltpu.VMEM)
SMEM = pl.BlockSpec(memory_space=pltpu.SMEM)


class Place:
    def __init__(self):
        self.columns = lax.axis_size("cp")
        self.group = lax.axis_size("grp")
        self.ring = self.group // 2
        self.half = self.ring // 2
        self.cp = lax.axis_index("cp")
        grp = lax.axis_index("grp")
        self.core = lax.rem(grp, 2)
        self.z = grp // 2
        self.turn = 1 - 2 * self.core
        self.ahead = (self.cp, self.place(1))
        self.behind = (self.cp, self.place(-1))
        self.later = (lax.rem(self.cp + 1, self.columns), grp)
        self.earlier = (lax.rem(self.cp + self.columns - 1, self.columns), grp)
        self.partner = (self.cp, 2 * self.z + 1 - self.core)
        self.peers = (self.ahead, self.behind, self.later, self.earlier, self.partner)

    def place(self, offset):
        return 2 * lax.rem(self.z + offset * self.turn + 2 * self.ring, self.ring) + self.core

    def far(self, offset):
        return self.place(offset)

    def near(self, offset):
        return self.group + self.place(offset)

    def greet(self):
        for peer in self.peers:
            pl.semaphore_signal(pltpu.get_barrier_semaphore(), inc=1, device_id=peer, device_id_type=MESH)

    def met(self):
        pl.semaphore_wait(pltpu.get_barrier_semaphore(), len(self.peers))


def slot_of(ids, count, j, cp, group):
    return jnp.clip(ids[0, j] - (cp - 1) * group, 0, 2 * group - 1)


def window_kernel(
    ids, count, seg_ref, key_any, value_any, query_any, grad_any,
    attended_any, dquery_any, dkey_any, dvalue_any,
    key_ref, value_ref, query_ref, grad_ref, attended_ref, dquery_ref, dkey_ref, dvalue_ref, bias, weights, dscores,
    meta, meta_in, other, out, inn, *rest,
):
    pools, terms, given = rest[:KV_HEADS], rest[KV_HEADS:2 * KV_HEADS], rest[2 * KV_HEADS:3 * KV_HEADS]
    gsend, grecv, psend, precv, rsend, rrecv, bsend, brecv, msend, mrecv, load, store, sload = rest[3 * KV_HEADS:]
    me = Place()
    half, ring, group = me.half, me.ring, me.group
    rows = key_ref.shape[0]
    head = key_ref.shape[1] // KV_HEADS
    width = query_ref.shape[1] // KV_HEADS
    listed = ids.shape[1]
    keys = listed * rows
    scaling = head ** (-0.5)

    me.greet()
    loads = [
        pltpu.make_async_copy(key_any, key_ref, load.at[2]),
        pltpu.make_async_copy(value_any, value_ref, load.at[3]),
        pltpu.make_async_copy(query_any, query_ref, load.at[0]),
        pltpu.make_async_copy(grad_any, grad_ref, load.at[1]),
    ]
    for what in loads:
        what.start()
    for h in range(KV_HEADS):
        terms[h][listed] = jnp.zeros((2 * rows, head), jnp.bfloat16)
        given[h][listed - 1] = jnp.zeros((2 * rows, head), jnp.bfloat16)

    slots = [slot_of(ids, count, j, me.cp, group) for j in range(listed)]
    mine = [jnp.where(j < count[0], slots[j], 2 * group) for j in range(listed)]
    lane = lax.broadcasted_iota(jnp.int32, meta.shape, 1)
    told = jnp.full(meta.shape, 2 * group, jnp.int32)
    for j in range(listed):
        told = jnp.where(lane == j, mine[j], told)
    meta[...] = told

    for what in loads[:2]:
        what.wait()

    above = [16] + [0] * (KV_HEADS - 1)
    own = me.near(0)
    pools[0][own, 0:16, :] = jnp.broadcast_to(seg_ref[...].astype(jnp.float32), (16, rows)).astype(jnp.bfloat16)
    for h in range(KV_HEADS):
        pools[h][own, above[h]:above[h] + rows, :] = key_ref[:, h * head:(h + 1) * head]
        pools[h][own, above[h] + rows:above[h] + 2 * rows, :] = value_ref[:, h * head:(h + 1) * head]

    me.met()

    def remote(source, target, send, recv, device):
        return pltpu.make_async_remote_copy(
            src_ref=source, dst_ref=target, send_sem=send, recv_sem=recv, device_id=device, device_id_type=MESH
        )

    started, shared = [], [[] for _ in range(KV_HEADS)]

    def start(what):
        what.start()
        started.append(what)

    def chain(flow, k, h):
        source, target, device = (
            (me.near(-k), me.near(-k), me.ahead),
            (me.near(-k), me.far(-k), me.later),
            (me.far(k), me.far(k), me.behind),
            (me.far(k), me.near(k), me.earlier),
        )[flow]
        return remote(pools[h].at[source], pools[h].at[target], gsend.at[flow, k, h], grecv.at[flow, k, h], device)

    def share(slot, h):
        n = len(shared[h])
        what = remote(pools[h].at[slot], pools[h].at[slot], psend.at[n, h], precv.at[n, h], me.partner)
        what.start()
        shared[h].append(what)

    def gather_hop(hop, h):
        if hop == 0:
            chain(1, 0, h).wait_recv()
            start(chain(2, 0, h))
        else:
            chain(2, hop - 1, h).wait_recv()
            if hop < half:
                start(chain(2, hop, h))
                start(chain(3, hop, h))
        if hop < half:
            chain(0, hop, h).wait_recv()
            if hop + 1 < half:
                start(chain(0, hop + 1, h))
                start(chain(1, hop + 1, h))
            share(me.near(-hop - 1), h)
        if hop >= 1:
            share(me.far(hop), h)
            if hop < half:
                chain(1, hop, h).wait_recv()
        if hop < half:
            share(me.far(-hop), h)
        if hop >= 2:
            chain(3, hop - 1, h).wait_recv()
            share(me.near(hop - 1), h)

    for h in range(KV_HEADS):
        start(chain(0, 0, h))
        start(chain(1, 0, h))
        share(own, h)
        if h == 0:
            meta_copy = remote(meta, meta_in, msend, mrecv, me.partner)
            meta_copy.start()
    for hop in range(half):
        for h in range(KV_HEADS):
            gather_hop(hop, h)
    for h in range(2):
        gather_hop(half, h)

    meta_copy.wait()
    meta_load = pltpu.make_async_copy(meta_in, other, sload)
    meta_load.start()
    for what in loads[2:]:
        what.wait()

    def dot(a, b, dims):
        return lax.dot_general(a, b, (dims, ((), ())), preferred_element_type=jnp.float32)

    across, plain = ((1,), (1,)), ((1,), (0,))

    transposed = {}

    def attend(h):
        for what in shared[h]:
            what.wait()
        pool, first = pools[h], above[h]
        if h == 0:
            asking = jnp.broadcast_to(seg_ref[...].astype(jnp.float32), (rows, rows))
            for j in range(listed):
                having = jnp.broadcast_to(pool[slots[j], 0:1, :].astype(jnp.float32), (rows, rows)).T
                live = jnp.where(j < count[0], 0.0, NEG)
                bias[j * rows:(j + 1) * rows, :] = jnp.where(asking == having, live, NEG)
        key = jnp.concatenate([pool[slots[j], first:first + rows, :] for j in range(listed)], axis=0)
        value = jnp.concatenate([pool[slots[j], first + rows:first + 2 * rows, :] for j in range(listed)], axis=0)
        transposed[h] = key.T, value.T
        heads = [slice(h * width + at, h * width + at + head) for at in range(0, width, head)]
        queries = [query_ref[:, at] for at in heads]
        grads = [grad_ref[:, at] for at in heads]
        for g in range(0, len(heads), 2):
            at = slice(g * head, (g + 2) * head)
            masked = jnp.concatenate([bias[...]] * 2, axis=1)
            scores = dot(key, jnp.concatenate(queries[g:g + 2], axis=0), across) + masked
            raised = jnp.exp((scores - jnp.max(scores, axis=0, keepdims=True)) * scaling)
            probability = raised * (1.0 / jnp.sum(raised, axis=0, keepdims=True))
            weight = probability.astype(jnp.bfloat16)
            dprobs = dot(value, jnp.concatenate(grads[g:g + 2], axis=0), across)
            delta = jnp.sum(weight.astype(jnp.float32) * dprobs, axis=0, keepdims=True)
            weights[h % 2, :, at] = weight
            dscores[h % 2, :, at] = (probability * (dprobs - delta)).astype(jnp.bfloat16)
        key_term = (dot(dscores[h % 2], jnp.concatenate(queries, axis=0), plain) * scaling).astype(jnp.bfloat16)
        value_term = dot(weights[h % 2], jnp.concatenate(grads, axis=0), plain).astype(jnp.bfloat16)
        for j in range(listed):
            terms[h][j, 0:rows, :] = key_term[j * rows:(j + 1) * rows, :]
            terms[h][j, rows:2 * rows, :] = value_term[j * rows:(j + 1) * rows, :]

    def finish(h):
        key_t, value_t = transposed.pop(h)
        attended = dot(value_t, weights[h % 2], plain).astype(jnp.bfloat16)
        dquery = (dot(key_t, dscores[h % 2], plain) * scaling).astype(jnp.bfloat16)
        for at in range(0, width, head):
            attended_ref[:, h * width + at:h * width + at + head] = attended[:, at:at + head].T
            dquery_ref[:, h * width + at:h * width + at + head] = dquery[:, at:at + head].T

    def mover(flow, k, h):
        at = k - 1 if flow in (0, 2) else k
        device = (me.behind, me.earlier, me.ahead, me.later)[flow]
        return remote(out.at[flow, at, h], inn.at[flow, at, h], rsend.at[flow, at, h], rrecv.at[flow, at, h], device)

    def total(slot, arrived, h):
        a, b = jnp.int32(listed), jnp.int32(listed - 1)
        for j in range(listed):
            a = jnp.where(mine[j] == slot, j, a)
        for j in range(1, listed):
            b = jnp.where(other[0, j] == slot, j - 1, b)
        sums = terms[h][a].astype(jnp.float32) + given[h][b].astype(jnp.float32)
        for flow, k in arrived:
            sums = sums + inn[flow, k, h].astype(jnp.float32)
        return sums.astype(jnp.bfloat16)

    def pass_on(flow, k, h, slot, arrived):
        out[flow, k - 1 if flow in (0, 2) else k, h] = total(slot, arrived, h)
        start(mover(flow, k, h))

    def arrival(flow, k, h):
        mover(flow, k + 1 if flow in (0, 2) else k, h).wait_recv()
        return flow, k

    gifts, stores = {}, []

    def put(n, h, a, b, columns):
        at = slice(h * columns, (h + 1) * columns)
        what = pltpu.make_async_copy(a.at[:, at], b.at[:, at], store.at[n, h])
        what.start()
        stores.append(what)

    def reduce(stage, h):
        if stage == 0:
            for j in range(1, listed):
                gifts[j, h] = remote(
                    terms[h].at[j], given[h].at[j - 1], bsend.at[j - 1, h], brecv.at[j - 1, h], me.partner
                )
                gifts[j, h].start()
        elif stage == 1:
            for j in range(1, listed):
                gifts[j, h].wait_recv()
            pass_on(0, half, h, me.near(-half), ())
            pass_on(2, half, h, me.far(half), ())
            for k in range(half - 1, 0, -1):
                pass_on(3, k, h, me.near(k), ())
                pass_on(1, k, h, me.far(-k), ())
            put(0, h, attended_ref, attended_any, width)
            put(1, h, dquery_ref, dquery_any, width)
        elif stage <= half:
            k = half + 1 - stage
            pass_on(2, k, h, me.far(k), (arrival(2, k, h), arrival(3, k, h)))
            pass_on(0, k, h, me.near(-k), (arrival(0, k, h), arrival(1, k, h)))
        elif stage == half + 1:
            pass_on(1, 0, h, me.far(0), (arrival(2, 0, h),))
        else:
            sums = total(me.near(0), (arrival(0, 0, h), arrival(1, 0, h)), h)
            dkey_ref[:, h * head:(h + 1) * head] = sums[0:rows, :]
            dvalue_ref[:, h * head:(h + 1) * head] = sums[rows:2 * rows, :]
            put(2, h, dkey_ref, dkey_any, head)
            put(3, h, dvalue_ref, dvalue_any, head)

    meta_load.wait()
    for turn in range(KV_HEADS + half + 2):
        if turn < KV_HEADS:
            attend(turn)
            reduce(0, turn)
            finish(turn)
            if turn + 2 < KV_HEADS:
                gather_hop(half, turn + 2)
            reduce(1, turn)
        for h in range(KV_HEADS - 1, -1, -1):
            if 2 <= turn - h <= half + 2:
                reduce(turn - h, h)
    for what in started:
        what.wait_send()
    for what in gifts.values():
        what.wait_send()
    for what in stores:
        what.wait()


def deliver_kernel(*refs):
    sources, targets, held, (load, store) = refs[:4], refs[4:8], refs[8:12], refs[12:]
    ins = [pltpu.make_async_copy(a, b, load.at[n]) for n, (a, b) in enumerate(zip(sources, held))]
    outs = [pltpu.make_async_copy(a, b, store.at[n]) for n, (a, b) in enumerate(zip(held, targets))]
    for what in ins:
        what.start()
    for a, b in zip(ins, outs):
        a.wait()
        b.start()
    for what in outs:
        what.wait()


def body(queries, keys, values, grad_out, segments, block_ids, block_count):
    rows = queries.shape[0]
    listed = block_ids.shape[1]
    head = keys.shape[1] // KV_HEADS
    width = queries.shape[1] // KV_HEADS
    group = lax.axis_size("grp")
    half = group // 4
    dma = pltpu.SemaphoreType.DMA
    vmem = functools.partial(pltpu.VMEM, dtype=jnp.bfloat16)
    anywhere = pl.BlockSpec(memory_space=pl.ANY)
    results = pl.pallas_call(
        window_kernel,
        out_shape=tuple(jax.ShapeDtypeStruct(a.shape, jnp.bfloat16) for a in (queries, queries, keys, values)),
        in_specs=[SMEM, SMEM, VMEM, anywhere, anywhere, anywhere, anywhere],
        out_specs=(anywhere,) * 4,
        scratch_shapes=[
            *[vmem(keys.shape)] * 2, *[vmem(queries.shape)] * 4, *[vmem(keys.shape)] * 2,
            pltpu.VMEM((listed * rows, rows), jnp.float32),
            vmem((2, listed * rows, width)),
            vmem((2, listed * rows, width)),
            pltpu.VMEM((8, 128), jnp.int32),
            pltpu.VMEM((8, 128), jnp.int32),
            pltpu.SMEM((8, 128), jnp.int32),
            vmem((4, half, KV_HEADS, 2 * rows, head)),
            vmem((4, half, KV_HEADS, 2 * rows, head)),
            vmem((2 * group, 2 * rows + 16, head)),
            *[vmem((2 * group, 2 * rows, head))] * (KV_HEADS - 1),
            *[vmem((listed + 1, 2 * rows, head))] * KV_HEADS,
            *[vmem((listed, 2 * rows, head))] * KV_HEADS,
            dma((4, half, KV_HEADS)), dma((4, half, KV_HEADS)),
            dma((group, KV_HEADS)), dma((group, KV_HEADS)),
            dma((4, half, KV_HEADS)), dma((4, half, KV_HEADS)),
            dma((listed - 1, KV_HEADS)), dma((listed - 1, KV_HEADS)),
            dma, dma, dma((4,)), dma((4, KV_HEADS)), dma,
        ],
        compiler_params=pltpu.CompilerParams(
            collective_id=0, has_side_effects=True, vmem_limit_bytes=60 * 1024 * 1024
        ),
        name="window",
    )(block_ids, block_count, segments.reshape(1, rows), keys, values, queries, grad_out)
    return pl.pallas_call(
        deliver_kernel,
        out_shape=tuple(jax.ShapeDtypeStruct(a.shape, a.dtype) for a in results),
        in_specs=[anywhere] * 4,
        out_specs=(anywhere,) * 4,
        scratch_shapes=[*[vmem(a.shape) for a in results], dma((4,)), dma((4,))],
        name="deliver",
    )(*results)


def solution(mesh):
    rows = P(("cp", "grp"), None)
    line = P(("cp", "grp"))
    return jax.shard_map(
        body,
        mesh=mesh,
        in_specs=(rows, rows, rows, rows, line, rows, line),
        out_specs=(rows, rows, rows, rows),
        check_vma=False,
    )
```
